512 devices in a mesh: dp: 8 (over z_hi, core), cuts: 16 (over y, x), topic: 4 (over z_lo).
Axes of the slice: x: 4, y: 4, z: 16 (z_hi: 4, z_lo: 4; z = z_hi * 4 + z_lo), core: 2. Of those that a mesh axis runs over, the one named last changes fastest.
Arguments:
- doc_mix: float32 [32768, 4096], P(('dp', 'cuts'), 'topic'), may hold values from 0.01 to 1
- doc_lengths: int32 [32768], P(('dp', 'cuts')), may hold values from 1 to 4096, 8388608 in all
- counts: int32 [32768, 1024], P(('dp', 'cuts')), may hold values from 0 to 7
- tile_on: int32 [128, 16], P(('dp', 'cuts')), may hold values from 0 to 1, as said below
- word_counts: float32 [1024, 4096], P('cuts', 'topic'), may hold values from 0.01 to 10
- topic_totals: float32 [4096], P('topic'), may hold values from 1000 to 100000
Outputs:
- doc_topic: float32 [32768, 4096], P(('dp', 'cuts'), 'topic')
- word_topic: float32 [1024, 4096], P('cuts', 'topic')
The draws below stay inside these ranges and needn't reach their ends.
Inputs may be any that keep to these rules, and one draw needn't show every extreme that they name: `tile_on`: each block of documents meets at least one word slice.
All inputs are finite; a program needn't handle non-finite values. No bound on the sum of `doc_lengths` on one device may be relied on, other than what follows from the above.
Results may differ from the reference program's by a relative error of at most 0.000078.
Values sent between devices are 32-bit elements; how exact they have to be, the bound alone decides.
No kernel may reach another device: no remote copies, remote signals or barrier semaphores. Data moves between devices by JAX's collectives and lax.ppermute only.
A program may use at most 64 MiB of HBM per device.

```python
import math
import jax
import jax.numpy as jnp
import numpy as np
from jax import lax

K = 4096
VOCAB = 1048576
WS = 64
DOC_DEV = 256
SLAB = 1024
DOC_BLOCKS = 128
DOCS = 32768
N_CUTS = 16


def draw_tile_on(key, part):
    level_key = jax.random.fold_in(key, 11)
    cell_key = jax.random.fold_in(key, 12)
    levels = jax.random.randint(level_key, (DOC_BLOCKS, 1), 2, 9)
    cells = jax.random.randint(cell_key, (DOC_BLOCKS, N_CUTS), 0, 8)
    rows = jnp.arange(DOC_BLOCKS, dtype=jnp.int32)[:, None]
    cols = jnp.arange(N_CUTS, dtype=jnp.int32)[None, :]
    forced = cols == rows % N_CUTS
    return jnp.where((cells < levels) | forced, 1, 0).astype(jnp.int32)


def place_ends(entries, stream_key, smallest, largest):
    longest = entries.shape.index(max(entries.shape))
    spots = []
    for shift in (0, 1):
        where = [jax.random.randint(jax.random.fold_in(stream_key, axis), (), 0, length) for axis, length in enumerate(entries.shape)]
        where[longest] = (where[longest] + shift) % entries.shape[longest]
        spots.append(tuple(where))
    return entries.at[spots[0]].set(smallest).at[spots[1]].set(largest)


def block_levels(stream_key, shape, cuts, smallest, largest):
    factor_of = 1.0
    for axis_at, blocks in cuts:
        heights = jax.random.uniform(jax.random.fold_in(jax.random.fold_in(stream_key, 6), axis_at), (blocks,), jnp.float32, smallest / len(cuts), largest / len(cuts))
        factor_of = factor_of * jnp.repeat(jnp.exp(heights), shape[axis_at] // blocks).reshape((-1,) + (1,) * (len(shape) - 1 - axis_at))
    return factor_of


def length_profile(count, total, reach, slope):
    portions = [(1 << 20) // math.isqrt(grade ** slope) + 1 for grade in range(2, count + 1)]
    surplus, given = total - reach - (count - 1), [1] * (count - 1)
    while surplus > 0:
        free = [i for i in range(count - 1) if given[i] < reach]
        whole, budget = sum([portions[i] for i in free]), surplus
        for i in free:
            more = min(reach - given[i], max(1, budget * portions[i] // whole), surplus)
            given[i] = given[i] + more
            surplus = surplus - more
    return np.array([reach] + given)


def ragged_sizes(own_key, number_of, total, limit, skew):
    if number_of == 2:
        one = jax.random.randint(own_key, (), max(1, total - limit), min(limit, total - 1) + 1)
        return jnp.stack([one, total - one])
    tallies = jnp.asarray(length_profile(number_of, total, limit, skew), jnp.int32)
    couples = (number_of - 1) // 2
    donor, taker = tallies[1:1 + 2 * couples:2], tallies[2:2 + 2 * couples:2]
    slack = jnp.minimum(donor - 1, limit - taker)
    passed = jax.random.randint(jax.random.fold_in(own_key, 1), (couples,), 0, 1 << 20) % (slack + 1)
    tallies = tallies.at[1:1 + 2 * couples:2].set(donor - passed).at[2:2 + 2 * couples:2].set(taker + passed)
    return tallies[jax.random.permutation(jax.random.fold_in(own_key, 2), number_of)]


def setup_inputs(seed: int = 0) -> dict:
    keys = jax.random.split(jax.random.key(seed), 7)
    doc_mix = jnp.clip(jnp.exp(math.log(1.0) - 4.6051702 * jax.random.uniform(keys[0], (DOCS, K), jnp.float32) ** block_levels(keys[0], (DOCS, K), ((0, 128), (1, 4)), -0.2, 0.2)), 0.01, 1.0)
    doc_lengths = ragged_sizes(keys[1], DOCS, 256 * DOCS, 4096, 2).astype(jnp.int32)
    counts = place_ends(jax.random.randint(keys[2], (DOCS, SLAB), 0, 8), jax.random.fold_in(keys[2], 1), 0, 7).astype(jnp.int32)
    tile_on = draw_tile_on(jax.random.fold_in(keys[6], 71), 0)
    word_counts = jnp.clip(jnp.exp(math.log(10.0) - 6.9077553 * jax.random.uniform(keys[4], (SLAB, K), jnp.float32) ** block_levels(keys[4], (SLAB, K), ((0, 16), (1, 4)), -0.2, 0.2)), 0.01, 10.0)
    topic_totals = jnp.clip(jnp.exp(math.log(100000.0) - 4.6051702 * jax.random.uniform(keys[5], (K,), jnp.float32) ** block_levels(keys[5], (K,), ((0, 4),), -0.2, 0.2)), 1000.0, 100000.0)
    return dict(doc_mix=doc_mix, doc_lengths=doc_lengths, counts=counts, tile_on=tile_on, word_counts=word_counts, topic_totals=topic_totals)


ALPHA = 0.1
BETA = 0.01


def reference(doc_mix, doc_lengths, counts, tile_on, word_counts, topic_totals):
    mass = jnp.sum(doc_mix, axis=1, keepdims=True)
    doc_weight = doc_lengths.astype(jnp.float32)[:, None] * doc_mix / mass + ALPHA
    word_weight = (word_counts + BETA) / (topic_totals + VOCAB * BETA)[None, :]
    tile_mask = jnp.repeat(jnp.repeat(tile_on, DOC_DEV, axis=0), WS, axis=1)
    weights = (counts * tile_mask).astype(jnp.float32)
    denom = jnp.dot(doc_weight, word_weight.T, precision=lax.Precision.HIGHEST, preferred_element_type=jnp.float32)
    ratio = weights / denom
    doc_topic = doc_weight * jnp.dot(ratio, word_weight, precision=lax.Precision.HIGHEST, preferred_element_type=jnp.float32)
    word_topic = word_weight * jnp.dot(ratio.T, doc_weight, precision=lax.Precision.HIGHEST, preferred_element_type=jnp.float32)
    return doc_topic, word_topic
```

```python
import jax
import jax.numpy as jnp
from jax import lax
from jax.sharding import Mesh, PartitionSpec as P

VOCAB = 1048576
ALPHA = 0.1
BETA = 0.01

CORES = 2
ROW_BLOCK = 8


def wrapped(place, size):
    return place & (size - 1)


def moved(block, axis, distance):
    size = lax.axis_size(axis)
    return lax.ppermute(block, axis, [(i, (i + distance) % size) for i in range(size)])


def gathered(block, axis):
    return jnp.concatenate([block] + [moved(block, axis, d) for d in range(1, lax.axis_size(axis))], axis=0)


def scattered(blocks, axis):
    total = blocks[0]
    for d in range(1, lax.axis_size(axis)):
        total = total + moved(blocks[d], axis, -d)
    return total


def matmul(left, right, contract):
    return lax.dot_general(left, right, (contract, ((), ())), precision=lax.Precision.HIGH, preferred_element_type=jnp.float32)


def shards(doc_mix, doc_lengths, counts, tile_on, word_counts, topic_totals):
    docs, topics = doc_mix.shape
    slice_words = word_counts.shape[0]
    n_zh, n_y, n_x, n_t = (lax.axis_size(a) for a in ("zh", "y", "x", "t"))
    core, y, x, t = (lax.axis_index(a) for a in ("core", "y", "x", "t"))
    half = slice_words // CORES

    scale = (topic_totals + VOCAB * BETA)[None, :]
    own_counts = lax.dynamic_index_in_dim(word_counts.reshape(n_zh, CORES, half // n_zh, topics), core, 1, False).reshape(half, topics)
    own_half = (own_counts + BETA) / scale
    words_here = gathered(gathered(own_half, "x"), "y")
    words_there = moved(words_here, "core", 1)

    mass = lax.psum(jnp.sum(doc_mix, axis=1), "t")
    doc_weight = doc_lengths.astype(jnp.float32)[:, None] * doc_mix / mass[:, None] + ALPHA

    tiles = jnp.repeat(tile_on[0], slice_words)[:, None]
    weights = (counts.T * tiles).astype(jnp.float32).reshape(n_y, n_x, n_zh, CORES, half // n_zh, docs)
    chunk = CORES * n_y * n_x * half // n_t
    per_chunk = chunk // half
    pieces = []
    for j in range(per_chunk):
        place = t * per_chunk + j
        dx, rest = wrapped(place, n_x), lax.div(place, n_x)
        dy, other = wrapped(rest, n_y), lax.div(rest, n_y)
        start = (wrapped(y - dy, n_y), wrapped(x - dx, n_x), 0, wrapped(core + other, CORES), 0, 0)
        piece = lax.dynamic_slice(weights, start, (1, 1, n_zh, 1, half // n_zh, docs))
        pieces.append(piece.reshape(half, docs))
    chunk_weights = jnp.concatenate(pieces, axis=0)

    by_topic = ((1,), (1,))
    partial = jnp.concatenate([matmul(words_here, doc_weight, by_topic), matmul(words_there, doc_weight, by_topic)], axis=0)
    denom = lax.dynamic_slice_in_dim(partial, t * chunk, chunk, 0)
    for d in range(1, n_t):
        denom = denom + moved(lax.dynamic_slice_in_dim(partial, wrapped(t + d, n_t) * chunk, chunk, 0), "t", d)
    chunk_ratio = chunk_weights / denom
    ratio = jnp.zeros((n_t * chunk, docs), jnp.float32)
    ratio = lax.dynamic_update_slice_in_dim(ratio, chunk_ratio, t * chunk, 0)
    for d in range(1, n_t):
        ratio = lax.dynamic_update_slice_in_dim(ratio, moved(chunk_ratio, "t", d), wrapped(t - d, n_t) * chunk, 0)

    middle = n_t * chunk // CORES
    ratio_here, ratio_there = ratio[:middle], ratio[middle:]
    sums_there = moved(matmul(ratio_there, doc_weight, ((1,), (0,))), "core", 1)
    sums = matmul(ratio_here, doc_weight, ((1,), (0,))) + sums_there
    sums = scattered(sums.reshape(n_y, n_x * half, topics), "y")
    sums = scattered(sums.reshape(n_x, half, topics), "x")
    zh = lax.axis_index("zh")
    rows = half // n_zh
    total = lax.dynamic_slice_in_dim(sums, zh * rows, rows, 0)
    for d in range(1, n_zh):
        total = total + moved(lax.dynamic_slice_in_dim(sums, wrapped(zh + d, n_zh) * rows, rows, 0), "zh", d)
    word_total = lax.all_gather(total, ("zh", "core"), tiled=True)

    by_word = ((0,), (0,))
    doc_sums = matmul(ratio_here, words_here, by_word) + matmul(ratio_there, words_there, by_word)
    return (doc_weight * doc_sums, (word_counts + BETA) / scale * word_total)


def solution(mesh):
    dp, cuts, topic = (mesh.shape[a] for a in ("dp", "cuts", "topic"))
    side = int(round(cuts**0.5))
    finer = Mesh(mesh.devices.reshape(dp // CORES, CORES, cuts // side, side, topic), ("zh", "core", "y", "x", "t"))
    docs, cut = ("zh", "core", "y", "x"), ("y", "x")
    return jax.shard_map(
        shards,
        mesh=finer,
        in_specs=(P(docs, "t"), P(docs), P(docs, None), P(docs, None), P(cut, "t"), P("t")),
        out_specs=(P(docs, "t"), P(cut, "t")),
        check_vma=False,
    )
```

```python
import jax
import jax.numpy as jnp
from jax import lax
from jax.sharding import Mesh, PartitionSpec as P


VOCAB = 1048576
ALPHA = 0.1
BETA = 0.01

CORES = 2
EXTRA = 8


def wrapped(place, size):
    return place & (size - 1)


def moved(block, axis, distance):
    size = lax.axis_size(axis)
    return lax.ppermute(block, axis, [(i, (i + distance) % size) for i in range(size)])


def exchanged(blocks, axes):
    return lax.all_to_all(blocks, axes, 0, 0, tiled=True)


def scattered(sums, axes):
    members = lax.axis_size(axes)
    rows = sums.shape[0] // members
    return jnp.sum(exchanged(sums, axes).reshape(members, rows, sums.shape[1]), axis=0)


def matmul(left, right, contract):
    return lax.dot_general(left, right, (contract, ((), ())), precision=lax.Precision.HIGH, preferred_element_type=jnp.float32)


def shards(doc_mix, doc_lengths, counts, tile_on, word_counts, topic_totals):
    docs, topics = doc_mix.shape
    slice_words = word_counts.shape[0]
    n_zh, n_t = lax.axis_size("zh"), lax.axis_size("t")
    cut = ("y", "x")
    n_cuts = lax.axis_size(cut)
    core, t = lax.axis_index("core"), lax.axis_index("t")
    half = slice_words // CORES
    rows = half // n_zh
    chunk = n_cuts * half // n_t

    scale = (topic_totals + VOCAB * BETA)[None, :]
    own_counts = lax.dynamic_index_in_dim(word_counts.reshape(n_zh, CORES, rows, topics), core, 1, False).reshape(half, topics)
    own_half = (own_counts + BETA) / scale
    copies = jnp.broadcast_to(own_half[None], (n_cuts, half, topics)).reshape(n_cuts * half, topics)
    words = [exchanged(copies, cut)]
    words.append(moved(words[0], "core", 1))

    tiles = jnp.repeat(tile_on[0], slice_words)[:, None]
    weights = (counts.T * tiles).astype(jnp.float32).reshape(n_cuts, n_zh, CORES, rows, docs)

    def chunk_weights(wave):
        start = (t * (n_cuts // n_t), 0, wrapped(core + wave, CORES), 0, 0)
        return lax.dynamic_slice(weights, start, (n_cuts // n_t, n_zh, 1, rows, docs)).reshape(chunk, docs)

    def parts_by_topic(wave, mix, extra):
        products = matmul(words[wave], mix, ((1,), (1,))).reshape(n_t, chunk, docs)
        word_sums = jnp.sum(words[wave], axis=1).reshape(n_t, 1, chunk)
        word_sums = jnp.pad(word_sums, ((0, 0), (0, EXTRA - 1 - len(extra)), (0, docs - chunk)))
        rows_below = [jnp.broadcast_to(row[None, None], (n_t, 1, docs)) for row in extra]
        return jnp.concatenate([products] + rows_below + [word_sums], axis=1)

    def sent_over_topics(blocks):
        return [moved(block, "t", d) for d, block in zip(range(1, n_t), blocks)]

    def by_owner(parts):
        return [lax.dynamic_index_in_dim(parts, wrapped(t + d, n_t), 0, False) for d in range(n_t)]

    def after(arrived, earlier):
        return lax.optimization_barrier((arrived, earlier))[0]

    def assembled(own, arrived):
        ratio = lax.dynamic_update_index_in_dim(jnp.zeros((n_t, chunk, docs), jnp.float32), own, t, 0)
        for d, block in zip(range(1, n_t), arrived):
            ratio = lax.dynamic_update_index_in_dim(ratio, block, wrapped(t - d, n_t), 0)
        return ratio.reshape(n_t * chunk, docs)

    by_doc = ((1,), (0,))
    parts_0 = parts_by_topic(0, doc_mix, [jnp.sum(doc_mix, axis=1)])
    own_0, *given_0 = by_owner(parts_0)
    arrived_0 = sent_over_topics(given_0)
    own_1, *given_1 = by_owner(parts_by_topic(1, after(doc_mix, parts_0), []))
    arrived_1 = sent_over_topics(given_1)

    total = own_0 + sum(after(arrived_0, given_1))
    doc_scale = doc_lengths.astype(jnp.float32) / total[chunk]
    doc_weight = doc_mix * doc_scale[:, None] + ALPHA
    chunk_0 = chunk_weights(0) / (total[:chunk] * doc_scale[None, :] + ALPHA * total[chunk + 1, :chunk][:, None])
    shared_0 = sent_over_topics([chunk_0] * (n_t - 1))

    total = own_1 + sum(after(arrived_1, chunk_0))
    chunk_1 = chunk_weights(1) / (total[:chunk] * doc_scale[None, :] + ALPHA * total[chunk, :chunk][:, None])
    shared_1 = sent_over_topics([chunk_1] * (n_t - 1))

    ratio_0 = assembled(chunk_0, after(shared_0, chunk_1))
    sums_0 = matmul(ratio_0, doc_weight, by_doc)
    ratio_1 = assembled(chunk_1, after(shared_1, sums_0))
    ratios = [ratio_0, ratio_1]

    sums_given = moved(sums_0, "core", 1)
    sums = scattered(matmul(ratios[1], doc_weight, by_doc) + sums_given, cut)
    sums = scattered(sums, "zh")
    word_total = lax.all_gather(sums, ("zh", "core"), tiled=True)
    word_total = word_total.reshape(n_zh, CORES, rows, topics)[:, ::-1].reshape(slice_words, topics)

    by_word = ((0,), (0,))
    doc_sums = matmul(ratios[0], words[0], by_word) + matmul(ratios[1], words[1], by_word)
    return (doc_weight * doc_sums, (word_counts + BETA) / scale * word_total)


def solution(mesh):
    dp, cuts, topic = (mesh.shape[a] for a in ("dp", "cuts", "topic"))
    side = int(round(cuts**0.5))
    finer = Mesh(mesh.devices.reshape(dp // CORES, CORES, cuts // side, side, topic), ("zh", "core", "y", "x", "t"))
    docs, cut = ("zh", "core", "y", "x"), ("y", "x")

    return jax.shard_map(
        shards,
        mesh=finer,
        in_specs=(P(docs, "t"), P(docs), P(docs, None), P(docs, None), P(cut, "t"), P("t")),
        out_specs=(P(docs, "t"), P(cut, "t")),
        check_vma=False,
    )
```

```python
import jax
import jax.numpy as jnp
from jax import lax
from jax.sharding import Mesh, PartitionSpec as P


VOCAB = 1048576
ALPHA = 0.1
BETA = 0.01

CORES = 2
EXTRA = 8


def wrapped(place, size):
    return place & (size - 1)


def moved(block, axis, partner):
    return lax.ppermute(block, axis, [(i, partner(i)) for i in range(lax.axis_size(axis))])


def after(arrived, earlier):
    return lax.optimization_barrier((arrived, earlier))[0]


def exchanged(blocks, axes):
    return lax.all_to_all(blocks, axes, 0, 0, tiled=True)


def scattered(sums, axes):
    members = lax.axis_size(axes)
    rows = sums.shape[0] // members
    return jnp.sum(exchanged(sums, axes).reshape(members, rows, sums.shape[1]), axis=0)


def matmul(left, right, contract):
    return lax.dot_general(left, right, (contract, ((), ())), precision=lax.Precision.HIGH, preferred_element_type=jnp.float32)


def first_partner(i):
    return i ^ 1


def second_partner(i):
    return i ^ 2


def across(i):
    return 3 - i


def joined(own, other, place):
    both = lax.dynamic_update_index_in_dim(jnp.zeros((2,) + own.shape, own.dtype), own, place, 0)
    return lax.dynamic_update_index_in_dim(both, other, 1 - place, 0).reshape((2 * own.shape[0],) + own.shape[1:])


def shards(doc_mix, doc_lengths, counts, tile_on, word_counts, topic_totals):
    docs, topics = doc_mix.shape
    slice_words = word_counts.shape[0]
    n_zh, n_t = lax.axis_size("zh"), lax.axis_size("t")
    cut = ("y", "x")
    n_cuts = lax.axis_size(cut)
    core, t = lax.axis_index("core"), lax.axis_index("t")
    half = slice_words // CORES
    rows = half // n_zh
    chunk = n_cuts * half // n_t
    low, high = t & 1, t >> 1
    quarter = 2 * low + high

    scale = (topic_totals + VOCAB * BETA)[None, :]
    own_counts = lax.dynamic_index_in_dim(word_counts.reshape(n_zh, CORES, rows, topics), core, 1, False).reshape(half, topics)
    own_half = (own_counts + BETA) / scale
    copies = jnp.broadcast_to(own_half[None], (n_cuts, half, topics)).reshape(n_cuts * half, topics)
    words = [exchanged(copies, cut)]
    words.append(moved(words[0], "core", first_partner))

    chunk_cuts = n_cuts // n_t
    chunk_counts = lax.dynamic_slice_in_dim(counts, quarter * (chunk_cuts * slice_words), chunk_cuts * slice_words, 1)
    chunk_tiles = lax.dynamic_slice_in_dim(tile_on[0], quarter * chunk_cuts, chunk_cuts, 0)
    weights = (chunk_counts.T * jnp.repeat(chunk_tiles, slice_words)[:, None]).astype(jnp.float32)
    weights = weights.reshape(chunk_cuts, n_zh, CORES, rows, docs)

    def chunk_weights(wave):
        return lax.dynamic_index_in_dim(weights, wrapped(core + wave, CORES), 2, False).reshape(chunk, docs)

    def parts_of(wave, mix):
        products = matmul(words[wave], mix, ((1,), (1,)))
        word_sums = matmul(jnp.ones((EXTRA - 1, topics), jnp.float32), words[wave], ((1,), (1,)))
        span = 2 * chunk
        halves = []
        for h in range(2):
            sums = jnp.pad(word_sums[:, h * span : (h + 1) * span], ((0, 0), (0, docs - span)))
            halves.append(jnp.concatenate([products[h * span : (h + 1) * span], mass_part, sums], axis=0))
        both = jnp.stack(halves)
        return lax.dynamic_index_in_dim(both, low, 0, False), lax.dynamic_index_in_dim(both, 1 - low, 0, False)

    def split(kept):
        chunks, extra = kept[: 2 * chunk].reshape(2, chunk, docs), kept[2 * chunk :]
        return [jnp.concatenate([lax.dynamic_index_in_dim(chunks, i, 0, False), extra], axis=0) for i in (high, 1 - high)]

    def ratio_of(wave, total, doc_scale):
        word_sums = lax.dynamic_slice_in_dim(total[chunk + 1], high * chunk, chunk, 0)
        return chunk_weights(wave) / (total[:chunk] * doc_scale[None, :] + ALPHA * word_sums[:, None])

    mass_part = jnp.sum(doc_mix, axis=1)[None, :]
    own_0, given_0 = parts_of(0, doc_mix)
    arrived_0 = moved(given_0, "t", first_partner)
    own_1, given_1 = parts_of(1, after(doc_mix, given_0))
    arrived_1 = moved(given_1, "t", first_partner)

    own_0, given_0 = split(own_0 + after(arrived_0, given_1))
    arrived_0 = moved(given_0, "t", second_partner)
    own_1, given_1 = split(own_1 + after(arrived_1, given_0))
    arrived_1 = moved(given_1, "t", second_partner)

    total = own_0 + after(arrived_0, given_1)
    doc_scale = doc_lengths.astype(jnp.float32) / total[chunk]
    doc_weight = doc_mix * doc_scale[:, None] + ALPHA
    chunk_0 = ratio_of(0, total, doc_scale)
    arrived_0 = moved(chunk_0, "t", second_partner)
    total = own_1 + after(arrived_1, chunk_0)
    chunk_1 = ratio_of(1, total, doc_scale)
    arrived_1 = moved(chunk_1, "t", second_partner)

    half_0 = joined(chunk_0, after(arrived_0, chunk_1), high)
    arrived_0 = moved(half_0, "t", first_partner)
    half_1 = joined(chunk_1, after(arrived_1, half_0), high)
    arrived_1 = moved(half_1, "t", first_partner)

    by_doc = ((1,), (0,))
    ratio_0 = joined(half_0, after(arrived_0, half_1), low)
    sums_0 = matmul(ratio_0, doc_weight, by_doc)
    sums_given = moved(sums_0, "core", first_partner)
    ratio_1 = joined(half_1, after(arrived_1, sums_0), low)

    sums = scattered(matmul(ratio_1, doc_weight, by_doc) + sums_given, cut)
    own_a, own_b = lax.optimization_barrier((sums[: half // 2], sums[half // 2 :]))
    arrived_a = moved(own_a, "zh", first_partner)
    arrived_b = moved(own_b, "zh", first_partner)
    own_a = own_a + arrived_a
    arrived_a = moved(own_a, "zh", across)
    own_b = own_b + after(arrived_b, own_a)
    arrived_b = moved(own_b, "zh", across)
    own_total = jnp.concatenate([own_a + arrived_a, own_b + arrived_b], axis=0)
    other_total = moved(own_total, "core", first_partner)
    own_total, other_total = (v.reshape(n_zh, 1, rows, topics) for v in (own_total, other_total))
    pair = (jnp.concatenate([other_total, own_total], axis=1), jnp.concatenate([own_total, other_total], axis=1))
    word_total = jnp.where(core == 0, *pair).reshape(slice_words, topics)

    by_word = ((0,), (0,))
    doc_sums = matmul(ratio_0, words[0], by_word) + matmul(ratio_1, words[1], by_word)
    return (doc_weight * doc_sums, (word_counts + BETA) / scale * word_total)


def solution(mesh):
    dp, cuts, topic = (mesh.shape[a] for a in ("dp", "cuts", "topic"))
    side = int(round(cuts**0.5))
    finer = Mesh(mesh.devices.reshape(dp // CORES, CORES, cuts // side, side, topic), ("zh", "core", "y", "x", "t"))
    docs, cut = ("zh", "core", "y", "x"), ("y", "x")

    return jax.shard_map(
        shards,
        mesh=finer,
        in_specs=(P(docs, "t"), P(docs), P(docs, None), P(docs, None), P(cut, "t"), P("t")),
        out_specs=(P(docs, "t"), P(cut, "t")),
        check_vma=False,
    )
```

```python
import jax
import jax.numpy as jnp
from jax import lax
from jax.sharding import Mesh, PartitionSpec as P


VOCAB = 1048576
ALPHA = 0.1
BETA = 0.01

CORES = 2
EXTRA = 8


def wrapped(place, size):
    return place & (size - 1)


def moved(block, axis, partner):
    return lax.ppermute(block, axis, [(i, partner(i)) for i in range(lax.axis_size(axis))])


def after(arrived, earlier):
    return lax.optimization_barrier((arrived, earlier))[0]


def exchanged(blocks, axes):
    return lax.all_to_all(blocks, axes, 0, 0, tiled=True)


def scattered(sums, axes):
    members = lax.axis_size(axes)
    rows = sums.shape[0] // members
    return jnp.sum(exchanged(sums, axes).reshape(members, rows, sums.shape[1]), axis=0)


def matmul(left, right, contract):
    return lax.dot_general(left, right, (contract, ((), ())), precision=lax.Precision.HIGH, preferred_element_type=jnp.float32)


def first_partner(i):
    return i ^ 1


def second_partner(i):
    return i ^ 2


def across(i):
    return 3 - i


def joined(own, other, place):
    both = lax.dynamic_update_index_in_dim(jnp.zeros((2,) + own.shape, own.dtype), own, place, 0)
    return lax.dynamic_update_index_in_dim(both, other, 1 - place, 0).reshape((2 * own.shape[0],) + own.shape[1:])


def shards(doc_mix, doc_lengths, counts, tile_on, word_counts, topic_totals):
    docs, topics = doc_mix.shape
    slice_words = word_counts.shape[0]
    n_zh, n_t = lax.axis_size("zh"), lax.axis_size("t")
    cut = ("y", "x")
    n_cuts = lax.axis_size(cut)
    core, t = lax.axis_index("core"), lax.axis_index("t")
    half = slice_words // CORES
    rows = half // n_zh
    chunk = n_cuts * half // n_t
    low, high = t & 1, t >> 1
    quarter = 2 * low + high

    scale = (topic_totals + VOCAB * BETA)[None, :]
    own_counts = lax.dynamic_index_in_dim(word_counts.reshape(n_zh, CORES, rows, topics), core, 1, False).reshape(half, topics)
    own_half = (own_counts + BETA) / scale
    copies = jnp.broadcast_to(own_half[None], (n_cuts, half, topics)).reshape(n_cuts * half, topics)
    words = [exchanged(copies, cut)]
    words.append(moved(words[0], "core", first_partner))

    chunk_cuts = n_cuts // n_t
    chunk_counts = lax.dynamic_slice_in_dim(counts, quarter * (chunk_cuts * slice_words), chunk_cuts * slice_words, 1)
    chunk_tiles = lax.dynamic_slice_in_dim(tile_on[0], quarter * chunk_cuts, chunk_cuts, 0)
    weights = (chunk_counts.T * jnp.repeat(chunk_tiles, slice_words)[:, None]).astype(jnp.float32)
    weights = weights.reshape(chunk_cuts, n_zh, CORES, rows, docs)

    def chunk_weights(wave):
        return lax.dynamic_index_in_dim(weights, wrapped(core + wave, CORES), 2, False).reshape(chunk, docs)

    def parts_of(wave, mix):
        products = matmul(words[wave], mix, ((1,), (1,))).reshape(n_t, chunk, docs)
        word_sums = jnp.sum(words[wave].reshape(n_cuts, half, topics), axis=2).reshape(n_t, 1, chunk)
        word_sums = jnp.pad(word_sums, ((0, 0), (0, EXTRA - 2), (0, docs - chunk)))
        parts = jnp.concatenate([products, jnp.broadcast_to(mass_part[None], (n_t, 1, docs)), word_sums], axis=1)
        return picked(parts.reshape(2, n_t // 2, chunk + EXTRA, docs), low)

    def picked(pair, place):
        return lax.dynamic_index_in_dim(pair, place, 0, False), lax.dynamic_index_in_dim(pair, 1 - place, 0, False)

    def ratio_of(wave, total, doc_scale):
        word_sums = total[chunk + 1, :chunk]
        return chunk_weights(wave) / (total[:chunk] * doc_scale[None, :] + ALPHA * word_sums[:, None])

    mass_part = jnp.sum(doc_mix, axis=1)[None, :]
    own_0, given_0 = parts_of(0, doc_mix)
    arrived_0 = moved(given_0, "t", first_partner)
    own_1, given_1 = parts_of(1, after(doc_mix, given_0))
    arrived_1 = moved(given_1, "t", first_partner)

    own_0, given_0 = picked(own_0 + after(arrived_0, given_1), high)
    arrived_0 = moved(given_0, "t", second_partner)
    own_1, given_1 = picked(own_1 + after(arrived_1, given_0), high)
    arrived_1 = moved(given_1, "t", second_partner)

    total = own_0 + after(arrived_0, given_1)
    doc_scale = doc_lengths.astype(jnp.float32) / total[chunk]
    doc_weight = doc_mix * doc_scale[:, None] + ALPHA
    chunk_0 = ratio_of(0, total, doc_scale)
    arrived_0 = moved(chunk_0, "t", second_partner)
    total = own_1 + after(arrived_1, chunk_0)
    chunk_1 = ratio_of(1, total, doc_scale)
    arrived_1 = moved(chunk_1, "t", second_partner)

    half_0 = joined(chunk_0, after(arrived_0, chunk_1), high)
    arrived_0 = moved(half_0, "t", first_partner)
    half_1 = joined(chunk_1, after(arrived_1, half_0), high)
    arrived_1 = moved(half_1, "t", first_partner)

    by_doc = ((1,), (0,))
    ratio_0 = joined(half_0, after(arrived_0, half_1), low)
    sums_0 = matmul(ratio_0, doc_weight, by_doc)
    sums_given = moved(sums_0, "core", first_partner)
    by_word = ((0,), (0,))
    doc_sums = matmul(ratio_0, words[0], by_word)
    ratio_1 = joined(half_1, after(arrived_1, doc_sums), low)

    sums = scattered(matmul(ratio_1, doc_weight, by_doc) + sums_given, cut)
    own_a, own_b = lax.optimization_barrier((sums[: half // 2], sums[half // 2 :]))
    arrived_a = moved(own_a, "zh", first_partner)
    arrived_b = moved(own_b, "zh", across)
    doc_topic = doc_weight * (doc_sums + matmul(ratio_1, words[1], by_word))
    own_a = own_a + after(arrived_a, doc_topic)
    arrived_a = moved(own_a, "zh", across)
    own_b = own_b + after(arrived_b, own_a)
    arrived_b = moved(own_b, "zh", first_partner)
    own_total = jnp.concatenate([own_a + arrived_a, own_b + arrived_b], axis=0)
    other_total = moved(own_total, "core", first_partner)
    own_total, other_total = (v.reshape(n_zh, 1, rows, topics) for v in (own_total, other_total))
    pair = (jnp.concatenate([other_total, own_total], axis=1), jnp.concatenate([own_total, other_total], axis=1))
    word_total = jnp.where(core == 0, *pair).reshape(slice_words, topics)

    return (doc_topic, (word_counts + BETA) / scale * word_total)


def solution(mesh):
    dp, cuts, topic = (mesh.shape[a] for a in ("dp", "cuts", "topic"))
    side = int(round(cuts**0.5))
    finer = Mesh(mesh.devices.reshape(dp // CORES, CORES, cuts // side, side, topic), ("zh", "core", "y", "x", "t"))
    docs, cut = ("zh", "core", "y", "x"), ("y", "x")

    return jax.shard_map(
        shards,
        mesh=finer,
        in_specs=(P(docs, "t"), P(docs), P(docs, None), P(docs, None), P(cut, "t"), P("t")),
        out_specs=(P(docs, "t"), P(cut, "t")),
        check_vma=False,
    )
```

```python
import jax
import jax.numpy as jnp
from jax import lax
from jax.experimental import pallas as pl
from jax.experimental.pallas import tpu as pltpu
from jax.sharding import Mesh, PartitionSpec as P


VOCAB = 1048576
ALPHA = 0.1
BETA = 0.01

CORES = 2
EXTRA = 8


def wrapped(place, size):
    return place & (size - 1)


def moved(block, axis, partner):
    return lax.ppermute(block, axis, [(i, partner(i)) for i in range(lax.axis_size(axis))])


def after(arrived, earlier):
    return lax.optimization_barrier((arrived, earlier))[0]


def exchanged(blocks, axes):
    return lax.all_to_all(blocks, axes, 0, 0, tiled=True)


def scattered(sums, axes):
    members = lax.axis_size(axes)
    rows = sums.shape[0] // members
    return jnp.sum(exchanged(sums, axes).reshape(members, rows, sums.shape[1]), axis=0)


def matmul(left, right, contract):
    return lax.dot_general(left, right, (contract, ((), ())), precision=lax.Precision.HIGH, preferred_element_type=jnp.float32)


def high_and_low(value):
    high = value.astype(jnp.bfloat16)
    return high, (value - high.astype(jnp.float32)).astype(jnp.bfloat16)


def parts_kernel(words_ref, mix_ref, mass_ref, parts_ref, mix_high, mix_low):
    @pl.when(pl.program_id(0) == 0)
    def _():
        mix_high[...], mix_low[...] = high_and_low(mix_ref[...])

    def product(left, right):
        return lax.dot_general(left, right, (((1,), (1,)), ((), ())), preferred_element_type=jnp.float32)

    chunk, topics = words_ref.shape
    docs = mass_ref.shape[1]
    words_high, words_low = high_and_low(words_ref[...])
    small = product(words_high, mix_low[...]) + product(words_low, mix_high[...])
    parts_ref[0, :chunk, :] = product(words_high, mix_high[...]) + small
    ones = jnp.ones((EXTRA, topics), jnp.bfloat16)
    word_sums = product(ones, words_high) + product(ones, words_low)
    word_sums = jnp.concatenate([word_sums, jnp.zeros((EXTRA, docs - chunk), jnp.float32)], axis=1)
    row = lax.broadcasted_iota(jnp.int32, (EXTRA, docs), 0)
    parts_ref[0, chunk:, :] = jnp.where(row == 0, mass_ref[...], word_sums)


def parts_of_words(words, mix, mass, chunks):
    docs, topics = mix.shape
    chunk = words.shape[0] // chunks
    return pl.pallas_call(
        parts_kernel,
        out_shape=jax.ShapeDtypeStruct((chunks, chunk + EXTRA, docs), jnp.float32),
        grid=(chunks,),
        in_specs=[
            pl.BlockSpec((chunk, topics), lambda i: (i, 0)),
            pl.BlockSpec((docs, topics), lambda i: (0, 0)),
            pl.BlockSpec((1, docs), lambda i: (0, 0)),
        ],
        out_specs=pl.BlockSpec((1, chunk + EXTRA, docs), lambda i: (i, 0, 0)),
        scratch_shapes=[pltpu.VMEM((docs, topics), jnp.bfloat16), pltpu.VMEM((docs, topics), jnp.bfloat16)],
        compiler_params=pltpu.CompilerParams(vmem_limit_bytes=16 * 2**20),
        cost_estimate=pl.CostEstimate(flops=6 * chunks * chunk * docs * topics, bytes_accessed=4 * topics * (docs + chunks * chunk), transcendentals=0),
    )(words, mix, mass)


def first_partner(i):
    return i ^ 1


def second_partner(i):
    return i ^ 2


def across(i):
    return 3 - i


def joined(own, other, place):
    both = lax.dynamic_update_index_in_dim(jnp.zeros((2,) + own.shape, own.dtype), own, place, 0)
    return lax.dynamic_update_index_in_dim(both, other, 1 - place, 0).reshape((2 * own.shape[0],) + own.shape[1:])


def shards(doc_mix, doc_lengths, counts, tile_on, word_counts, topic_totals):
    docs, topics = doc_mix.shape
    slice_words = word_counts.shape[0]
    n_zh, n_t = lax.axis_size("zh"), lax.axis_size("t")
    cut = ("y", "x")
    n_cuts = lax.axis_size(cut)
    core, t = lax.axis_index("core"), lax.axis_index("t")
    half = slice_words // CORES
    rows = half // n_zh
    chunk = n_cuts * half // n_t
    low, high = t & 1, t >> 1
    quarter = 2 * low + high

    scale = (topic_totals + VOCAB * BETA)[None, :]
    own_counts = lax.dynamic_index_in_dim(word_counts.reshape(n_zh, CORES, rows, topics), core, 1, False).reshape(half, topics)
    own_half = (own_counts + BETA) / scale
    copies = jnp.broadcast_to(own_half[None], (n_cuts, half, topics)).reshape(n_cuts * half, topics)
    words = [exchanged(copies, cut)]
    words.append(moved(words[0], "core", first_partner))

    chunk_cuts = n_cuts // n_t
    chunk_counts = lax.dynamic_slice_in_dim(counts, quarter * (chunk_cuts * slice_words), chunk_cuts * slice_words, 1)
    chunk_tiles = lax.dynamic_slice_in_dim(tile_on[0], quarter * chunk_cuts, chunk_cuts, 0)
    weights = (chunk_counts.T * jnp.repeat(chunk_tiles, slice_words)[:, None]).astype(jnp.float32)
    weights = weights.reshape(chunk_cuts, n_zh, CORES, rows, docs)

    def chunk_weights(wave):
        return lax.dynamic_index_in_dim(weights, wrapped(core + wave, CORES), 2, False).reshape(chunk, docs)

    def parts_of(wave, mix):
        parts = parts_of_words(words[wave], mix, mass_part, n_t)
        return picked(parts.reshape(2, n_t // 2, chunk + EXTRA, docs), low)

    def picked(pair, place):
        return lax.dynamic_index_in_dim(pair, place, 0, False), lax.dynamic_index_in_dim(pair, 1 - place, 0, False)

    def ratio_of(wave, total, doc_scale):
        word_sums = total[chunk + 1, :chunk]
        return chunk_weights(wave) / (total[:chunk] * doc_scale[None, :] + ALPHA * word_sums[:, None])

    mass_part = jnp.sum(doc_mix, axis=1)[None, :]
    own_0, given_0 = parts_of(0, doc_mix)
    arrived_0 = moved(given_0, "t", first_partner)
    own_1, given_1 = parts_of(1, after(doc_mix, given_0))
    arrived_1 = moved(given_1, "t", first_partner)

    own_0, given_0 = picked(own_0 + after(arrived_0, given_1), high)
    arrived_0 = moved(given_0, "t", second_partner)
    own_1, given_1 = picked(own_1 + after(arrived_1, given_0), high)
    arrived_1 = moved(given_1, "t", second_partner)

    total = own_0 + after(arrived_0, given_1)
    doc_scale = doc_lengths.astype(jnp.float32) / total[chunk]
    doc_weight = doc_mix * doc_scale[:, None] + ALPHA
    chunk_0 = ratio_of(0, total, doc_scale)
    arrived_0 = moved(chunk_0, "t", second_partner)
    total = own_1 + after(arrived_1, chunk_0)
    chunk_1 = ratio_of(1, total, doc_scale)
    arrived_1 = moved(chunk_1, "t", second_partner)

    half_0 = joined(chunk_0, after(arrived_0, chunk_1), high)
    arrived_0 = moved(half_0, "t", first_partner)
    half_1 = joined(chunk_1, after(arrived_1, half_0), high)
    arrived_1 = moved(half_1, "t", first_partner)

    by_doc = ((1,), (0,))
    ratio_0 = joined(half_0, after(arrived_0, half_1), low)
    sums_0 = matmul(ratio_0, doc_weight, by_doc)
    sums_given = moved(sums_0, "core", first_partner)
    by_word = ((0,), (0,))
    doc_sums = matmul(ratio_0, words[0], by_word)
    ratio_1 = joined(half_1, after(arrived_1, doc_sums), low)

    sums = scattered(matmul(ratio_1, doc_weight, by_doc) + sums_given, cut)
    own_a, own_b = lax.optimization_barrier((sums[: half // 2], sums[half // 2 :]))
    arrived_a = moved(own_a, "zh", first_partner)
    arrived_b = moved(own_b, "zh", across)
    doc_topic = doc_weight * (doc_sums + matmul(ratio_1, words[1], by_word))
    own_a = own_a + after(arrived_a, doc_topic)
    arrived_a = moved(own_a, "zh", across)
    own_b = own_b + after(arrived_b, own_a)
    arrived_b = moved(own_b, "zh", first_partner)
    own_total = jnp.concatenate([own_a + arrived_a, own_b + arrived_b], axis=0)
    other_total = moved(own_total, "core", first_partner)
    own_total, other_total = (v.reshape(n_zh, 1, rows, topics) for v in (own_total, other_total))
    pair = (jnp.concatenate([other_total, own_total], axis=1), jnp.concatenate([own_total, other_total], axis=1))
    word_total = jnp.where(core == 0, *pair).reshape(slice_words, topics)

    return (doc_topic, (word_counts + BETA) / scale * word_total)


def solution(mesh):
    dp, cuts, topic = (mesh.shape[a] for a in ("dp", "cuts", "topic"))
    side = int(round(cuts**0.5))
    finer = Mesh(mesh.devices.reshape(dp // CORES, CORES, cuts // side, side, topic), ("zh", "core", "y", "x", "t"))
    docs, cut = ("zh", "core", "y", "x"), ("y", "x")

    return jax.shard_map(
        shards,
        mesh=finer,
        in_specs=(P(docs, "t"), P(docs), P(docs, None), P(docs, None), P(cut, "t"), P("t")),
        out_specs=(P(docs, "t"), P(cut, "t")),
        check_vma=False,
    )
```

```python
import jax
import jax.numpy as jnp
from jax import lax
from jax.experimental import pallas as pl
from jax.experimental.pallas import tpu as pltpu
from jax.sharding import Mesh, PartitionSpec as P


VOCAB = 1048576
ALPHA = 0.1
BETA = 0.01

CORES = 2
EXTRA = 8
STEPS = 2


def wrapped(place, size):
    return place & (size - 1)


def moved(block, axis, partner):
    return lax.ppermute(block, axis, [(i, partner(i)) for i in range(lax.axis_size(axis))])


def after(arrived, earlier):
    return lax.optimization_barrier((arrived, earlier))[0]


def exchanged(blocks, axes):
    return lax.all_to_all(blocks, axes, 0, 0, tiled=True)


def scattered(sums, axes):
    members = lax.axis_size(axes)
    rows = sums.shape[0] // members
    return jnp.sum(exchanged(sums, axes).reshape(members, rows, sums.shape[1]), axis=0)


def matmul(left, right, contract):
    return lax.dot_general(left, right, (contract, ((), ())), precision=lax.Precision.HIGH, preferred_element_type=jnp.float32)


def high_and_low(value):
    high = value.astype(jnp.bfloat16)
    return high, (value - high.astype(jnp.float32)).astype(jnp.bfloat16)


def parts_kernel(words_ref, mix_ref, mass_ref, parts_ref):
    def product(left, right):
        return lax.dot_general(left, right, (((1,), (1,)), ((), ())), preferred_element_type=jnp.float32)

    chunks, rows, docs = parts_ref.shape
    chunk = rows - EXTRA
    first = pl.program_id(0) == 0

    @pl.when(first)
    def _():
        parts_ref[...] = jnp.zeros_like(parts_ref)

    mix_high, mix_low = high_and_low(mix_ref[...])
    words_high, words_low = high_and_low(words_ref[...])
    products = product(words_high, mix_low) + product(words_low, mix_high) + product(words_high, mix_high)
    diagonal = lax.broadcasted_iota(jnp.int32, (chunk, chunk), 0) == lax.broadcasted_iota(jnp.int32, (chunk, chunk), 1)
    row = lax.broadcasted_iota(jnp.int32, (EXTRA, docs), 0)
    mass = jnp.where(first, mass_ref[...], 0.0)
    for c in range(chunks):
        span = slice(c * chunk, (c + 1) * chunk)
        sums = jnp.sum(words_ref[span, :], axis=1, keepdims=True)
        sums = jnp.sum(jnp.where(diagonal, sums, 0.0), axis=0, keepdims=True)
        sums = jnp.concatenate([sums, jnp.zeros((1, docs - chunk), jnp.float32)], axis=1)
        parts_ref[c, :chunk, :] += products[span]
        parts_ref[c, chunk:, :] += jnp.where(row == 0, mass, sums)


def parts_of_words(words, mix, mass, chunks):
    docs, topics = mix.shape
    chunk = words.shape[0] // chunks
    return pl.pallas_call(
        parts_kernel,
        out_shape=jax.ShapeDtypeStruct((chunks, chunk + EXTRA, docs), jnp.float32),
        grid=(STEPS,),
        in_specs=[
            pl.BlockSpec((chunks * chunk, topics // STEPS), lambda i: (0, i)),
            pl.BlockSpec((docs, topics // STEPS), lambda i: (0, i)),
            pl.BlockSpec((1, docs), lambda i: (0, 0)),
        ],
        out_specs=pl.BlockSpec((chunks, chunk + EXTRA, docs), lambda i: (0, 0, 0)),
        compiler_params=pltpu.CompilerParams(vmem_limit_bytes=24 * 2**20),
        cost_estimate=pl.CostEstimate(flops=6 * chunks * chunk * docs * topics, bytes_accessed=4 * topics * (docs + chunks * chunk), transcendentals=0),
    )(words, mix, mass)


def first_partner(i):
    return i ^ 1


def second_partner(i):
    return i ^ 2


def across(i):
    return 3 - i


def joined(own, other, place):
    both = lax.dynamic_update_index_in_dim(jnp.zeros((2,) + own.shape, own.dtype), own, place, 0)
    return lax.dynamic_update_index_in_dim(both, other, 1 - place, 0).reshape((2 * own.shape[0],) + own.shape[1:])


def shards(doc_mix, doc_lengths, counts, tile_on, word_counts, topic_totals):
    docs, topics = doc_mix.shape
    slice_words = word_counts.shape[0]
    n_zh, n_t = lax.axis_size("zh"), lax.axis_size("t")
    cut = ("y", "x")
    n_cuts = lax.axis_size(cut)
    core, t = lax.axis_index("core"), lax.axis_index("t")
    half = slice_words // CORES
    rows = half // n_zh
    chunk = n_cuts * half // n_t
    low, high = t & 1, t >> 1
    quarter = 2 * low + high

    scale = (topic_totals + VOCAB * BETA)[None, :]
    own_counts = lax.dynamic_index_in_dim(word_counts.reshape(n_zh, CORES, rows, topics), core, 1, False).reshape(half, topics)
    own_half = (own_counts + BETA) / scale
    copies = jnp.broadcast_to(own_half[None], (n_cuts, half, topics)).reshape(n_cuts * half, topics)
    words = [exchanged(copies, cut)]
    words.append(moved(words[0], "core", first_partner))

    chunk_cuts = n_cuts // n_t
    chunk_counts = lax.dynamic_slice_in_dim(counts, quarter * (chunk_cuts * slice_words), chunk_cuts * slice_words, 1)
    chunk_tiles = lax.dynamic_slice_in_dim(tile_on[0], quarter * chunk_cuts, chunk_cuts, 0)
    weights = (chunk_counts.T * jnp.repeat(chunk_tiles, slice_words)[:, None]).astype(jnp.float32)
    weights = weights.reshape(chunk_cuts, n_zh, CORES, rows, docs)

    def chunk_weights(wave):
        return lax.dynamic_index_in_dim(weights, wrapped(core + wave, CORES), 2, False).reshape(chunk, docs)

    def parts_of(wave, mix):
        parts = parts_of_words(words[wave], mix, mass_part, n_t)
        return picked(parts.reshape(2, n_t // 2, chunk + EXTRA, docs), low)

    def picked(pair, place):
        return lax.dynamic_index_in_dim(pair, place, 0, False), lax.dynamic_index_in_dim(pair, 1 - place, 0, False)

    def ratio_of(wave, total, doc_scale):
        word_sums = total[chunk + 1, :chunk]
        return chunk_weights(wave) / (total[:chunk] * doc_scale[None, :] + ALPHA * word_sums[:, None])

    mass_part = jnp.sum(doc_mix, axis=1)[None, :]
    own_0, given_0 = parts_of(0, doc_mix)
    arrived_0 = moved(given_0, "t", first_partner)
    own_1, given_1 = parts_of(1, after(doc_mix, given_0))
    arrived_1 = moved(given_1, "t", first_partner)

    own_0, given_0 = picked(own_0 + after(arrived_0, given_1), high)
    arrived_0 = moved(given_0, "t", second_partner)
    own_1, given_1 = picked(own_1 + after(arrived_1, given_0), high)
    arrived_1 = moved(given_1, "t", second_partner)

    total = own_0 + after(arrived_0, given_1)
    doc_scale = doc_lengths.astype(jnp.float32) / total[chunk]
    doc_weight = doc_mix * doc_scale[:, None] + ALPHA
    chunk_0 = ratio_of(0, total, doc_scale)
    arrived_0 = moved(chunk_0, "t", second_partner)
    total = own_1 + after(arrived_1, chunk_0)
    chunk_1 = ratio_of(1, total, doc_scale)
    arrived_1 = moved(chunk_1, "t", second_partner)

    half_0 = joined(chunk_0, after(arrived_0, chunk_1), high)
    arrived_0 = moved(half_0, "t", first_partner)
    half_1 = joined(chunk_1, after(arrived_1, half_0), high)
    arrived_1 = moved(half_1, "t", first_partner)

    by_doc = ((1,), (0,))
    ratio_0 = joined(half_0, after(arrived_0, half_1), low)
    sums_0 = matmul(ratio_0, doc_weight, by_doc)
    sums_given = moved(sums_0, "core", first_partner)
    by_word = ((0,), (0,))
    doc_sums = matmul(ratio_0, words[0], by_word)
    ratio_1 = joined(half_1, after(arrived_1, doc_sums), low)

    sums = scattered(matmul(ratio_1, doc_weight, by_doc) + sums_given, cut)
    own_a, own_b = lax.optimization_barrier((sums[: half // 2], sums[half // 2 :]))
    arrived_a = moved(own_a, "zh", first_partner)
    arrived_b = moved(own_b, "zh", across)
    doc_topic = doc_weight * (doc_sums + matmul(ratio_1, words[1], by_word))
    own_a = own_a + after(arrived_a, doc_topic)
    arrived_a = moved(own_a, "zh", across)
    own_b = own_b + after(arrived_b, own_a)
    arrived_b = moved(own_b, "zh", first_partner)
    own_total = jnp.concatenate([own_a + arrived_a, own_b + arrived_b], axis=0)
    other_total = moved(own_total, "core", first_partner)
    own_total, other_total = (v.reshape(n_zh, 1, rows, topics) for v in (own_total, other_total))
    pair = (jnp.concatenate([other_total, own_total], axis=1), jnp.concatenate([own_total, other_total], axis=1))
    word_total = jnp.where(core == 0, *pair).reshape(slice_words, topics)

    return (doc_topic, (word_counts + BETA) / scale * word_total)


def solution(mesh):
    dp, cuts, topic = (mesh.shape[a] for a in ("dp", "cuts", "topic"))
    side = int(round(cuts**0.5))
    finer = Mesh(mesh.devices.reshape(dp // CORES, CORES, cuts // side, side, topic), ("zh", "core", "y", "x", "t"))
    docs, cut = ("zh", "core", "y", "x"), ("y", "x")

    return jax.shard_map(
        shards,
        mesh=finer,
        in_specs=(P(docs, "t"), P(docs), P(docs, None), P(docs, None), P(cut, "t"), P("t")),
        out_specs=(P(docs, "t"), P(cut, "t")),
        check_vma=False,
    )
```

```python
import jax
import jax.numpy as jnp
from jax import lax
from jax.experimental import pallas as pl
from jax.experimental.pallas import tpu as pltpu
from jax.sharding import Mesh, PartitionSpec as P


VOCAB = 1048576
ALPHA = 0.1
BETA = 0.01

CORES = 2
EXTRA = 8
STEPS = 2


def wrapped(place, size):
    return place & (size - 1)


def moved(block, axis, partner):
    return lax.ppermute(block, axis, [(i, partner(i)) for i in range(lax.axis_size(axis))])


def after(arrived, earlier):
    return lax.optimization_barrier((arrived, earlier))[0]


def exchanged(blocks, axes):
    return lax.all_to_all(blocks, axes, 0, 0, tiled=True)


def scattered(sums, axes):
    members = lax.axis_size(axes)
    rows = sums.shape[0] // members
    return jnp.sum(exchanged(sums, axes).reshape(members, rows, sums.shape[1]), axis=0)


def matmul(left, right, contract):
    return lax.dot_general(left, right, (contract, ((), ())), precision=lax.Precision.HIGH, preferred_element_type=jnp.float32)


def high_and_low(value):
    high = value.astype(jnp.bfloat16)
    return high, (value - high.astype(jnp.float32)).astype(jnp.bfloat16)


def parts_kernel(words_ref, mix_ref, mass_ref, parts_ref):
    def product(left, right):
        return lax.dot_general(left, right, (((1,), (1,)), ((), ())), preferred_element_type=jnp.float32)

    chunks, rows, docs = parts_ref.shape
    chunk = rows - EXTRA
    first = pl.program_id(0) == 0

    @pl.when(first)
    def _():
        parts_ref[...] = jnp.zeros_like(parts_ref)

    mix_high, mix_low = high_and_low(mix_ref[...])
    words_high, words_low = high_and_low(words_ref[...])
    products = product(words_high, mix_low) + product(words_low, mix_high) + product(words_high, mix_high)
    diagonal = lax.broadcasted_iota(jnp.int32, (chunk, chunk), 0) == lax.broadcasted_iota(jnp.int32, (chunk, chunk), 1)
    row = lax.broadcasted_iota(jnp.int32, (EXTRA, docs), 0)
    mass = jnp.where(first, mass_ref[...], 0.0)
    for c in range(chunks):
        span = slice(c * chunk, (c + 1) * chunk)
        sums = jnp.sum(words_ref[span, :], axis=1, keepdims=True)
        sums = jnp.sum(jnp.where(diagonal, sums, 0.0), axis=0, keepdims=True)
        sums = jnp.concatenate([sums, jnp.zeros((1, docs - chunk), jnp.float32)], axis=1)
        parts_ref[c, :chunk, :] += products[span]
        parts_ref[c, chunk:, :] += jnp.where(row == 0, mass, sums)


def parts_of_words(words, mix, mass, chunks):
    docs, topics = mix.shape
    chunk = words.shape[0] // chunks
    return pl.pallas_call(
        parts_kernel,
        out_shape=jax.ShapeDtypeStruct((chunks, chunk + EXTRA, docs), jnp.float32),
        grid=(STEPS,),
        in_specs=[
            pl.BlockSpec((chunks * chunk, topics // STEPS), lambda i: (0, i)),
            pl.BlockSpec((docs, topics // STEPS), lambda i: (0, i)),
            pl.BlockSpec((1, docs), lambda i: (0, 0)),
        ],
        out_specs=pl.BlockSpec((chunks, chunk + EXTRA, docs), lambda i: (0, 0, 0)),
        compiler_params=pltpu.CompilerParams(vmem_limit_bytes=24 * 2**20),
        cost_estimate=pl.CostEstimate(flops=6 * chunks * chunk * docs * topics, bytes_accessed=4 * topics * (docs + chunks * chunk), transcendentals=0),
    )(words, mix, mass)


def first_partner(i):
    return i ^ 1


def second_partner(i):
    return i ^ 2


def across(i):
    return 3 - i


def joined(own, other, place):
    both = lax.dynamic_update_index_in_dim(jnp.zeros((2,) + own.shape, own.dtype), own, place, 0)
    return lax.dynamic_update_index_in_dim(both, other, 1 - place, 0).reshape((2 * own.shape[0],) + own.shape[1:])


def shards(doc_mix, doc_lengths, counts, tile_on, word_counts, topic_totals):
    docs, topics = doc_mix.shape
    slice_words = word_counts.shape[0]
    n_zh, n_t = lax.axis_size("zh"), lax.axis_size("t")
    cut = ("y", "x")
    n_cuts = lax.axis_size(cut)
    core, t = lax.axis_index("core"), lax.axis_index("t")
    half = slice_words // CORES
    rows = half // n_zh
    chunk = n_cuts * half // n_t
    low, high = t & 1, t >> 1
    quarter = 2 * low + high

    scale = (topic_totals + VOCAB * BETA)[None, :]
    own_counts = lax.dynamic_index_in_dim(word_counts.reshape(n_zh, CORES, rows, topics), core, 1, False).reshape(half, topics)
    own_half = (own_counts + BETA) / scale
    copies = jnp.broadcast_to(own_half[None], (n_cuts, half, topics)).reshape(n_cuts * half, topics)
    words = [exchanged(copies, cut)]
    words.append(moved(words[0], "core", first_partner))

    chunk_cuts = n_cuts // n_t
    chunk_counts = lax.dynamic_slice_in_dim(counts, quarter * (chunk_cuts * slice_words), chunk_cuts * slice_words, 1)
    chunk_tiles = lax.dynamic_slice_in_dim(tile_on[0], quarter * chunk_cuts, chunk_cuts, 0)
    weights = (chunk_counts.T * jnp.repeat(chunk_tiles, slice_words)[:, None]).astype(jnp.float32)
    weights = weights.reshape(chunk_cuts, n_zh, CORES, rows, docs)

    def chunk_weights(wave):
        return lax.dynamic_index_in_dim(weights, wrapped(core + wave, CORES), 2, False).reshape(chunk, docs)

    def parts_of(wave, mix):
        parts = parts_of_words(words[wave], mix, mass_part, n_t)
        return picked(parts.reshape(2, n_t // 2, chunk + EXTRA, docs), low)

    def picked(pair, place):
        return lax.dynamic_index_in_dim(pair, place, 0, False), lax.dynamic_index_in_dim(pair, 1 - place, 0, False)

    def ratio_of(wave, total, doc_scale):
        word_sums = total[chunk + 1, :chunk]
        return chunk_weights(wave) / (total[:chunk] * doc_scale[None, :] + ALPHA * word_sums[:, None])

    mass_part = jnp.sum(doc_mix, axis=1)[None, :]
    own_0, given_0 = parts_of(0, doc_mix)
    arrived_0 = moved(given_0, "t", first_partner)
    own_1, given_1 = parts_of(1, after(doc_mix, given_0))
    arrived_1 = moved(given_1, "t", first_partner)

    own_0, given_0 = picked(own_0 + after(arrived_0, given_1), high)
    arrived_0 = moved(given_0, "t", second_partner)
    own_1, given_1 = picked(own_1 + after(arrived_1, given_0), high)
    arrived_1 = moved(given_1, "t", second_partner)

    total = own_0 + after(arrived_0, given_1)
    doc_scale = doc_lengths.astype(jnp.float32) / total[chunk]
    doc_weight = doc_mix * doc_scale[:, None] + ALPHA
    chunk_0 = ratio_of(0, total, doc_scale)
    arrived_0 = moved(chunk_0, "t", second_partner)
    total = own_1 + after(arrived_1, chunk_0)
    chunk_1 = ratio_of(1, total, doc_scale)
    arrived_1 = moved(chunk_1, "t", second_partner)

    half_0 = joined(chunk_0, after(arrived_0, chunk_1), high)
    arrived_0 = moved(half_0, "t", first_partner)
    half_1 = joined(chunk_1, after(arrived_1, half_0), high)
    arrived_1 = moved(half_1, "t", first_partner)

    by_doc = ((1,), (0,))
    ratio_0 = joined(half_0, after(arrived_0, half_1), low)
    sums_0 = matmul(ratio_0, doc_weight, by_doc)
    sums_given = moved(sums_0, "core", first_partner)
    by_word = ((0,), (0,))
    ratio_1 = joined(half_1, after(arrived_1, sums_0), low)

    sums = scattered(matmul(ratio_1, doc_weight, by_doc) + sums_given, cut)
    own_a, own_b = lax.optimization_barrier((sums[: half // 2], sums[half // 2 :]))
    arrived_a = moved(own_a, "zh", first_partner)
    arrived_b = moved(own_b, "zh", across)
    doc_topic = doc_weight * (matmul(ratio_0, words[0], by_word) + matmul(ratio_1, words[1], by_word))
    own_a = own_a + after(arrived_a, doc_topic)
    arrived_a = moved(own_a, "zh", across)
    own_b = own_b + after(arrived_b, own_a)
    arrived_b = moved(own_b, "zh", first_partner)
    own_total = jnp.concatenate([own_a + arrived_a, own_b + arrived_b], axis=0)
    other_total = moved(own_total, "core", first_partner)
    own_total, other_total = (v.reshape(n_zh, 1, rows, topics) for v in (own_total, other_total))
    pair = (jnp.concatenate([other_total, own_total], axis=1), jnp.concatenate([own_total, other_total], axis=1))
    word_total = jnp.where(core == 0, *pair).reshape(slice_words, topics)

    return (doc_topic, (word_counts + BETA) / scale * word_total)


def solution(mesh):
    dp, cuts, topic = (mesh.shape[a] for a in ("dp", "cuts", "topic"))
    side = int(round(cuts**0.5))
    finer = Mesh(mesh.devices.reshape(dp // CORES, CORES, cuts // side, side, topic), ("zh", "core", "y", "x", "t"))
    docs, cut = ("zh", "core", "y", "x"), ("y", "x")

    return jax.shard_map(
        shards,
        mesh=finer,
        in_specs=(P(docs, "t"), P(docs), P(docs, None), P(docs, None), P(cut, "t"), P("t")),
        out_specs=(P(docs, "t"), P(cut, "t")),
        check_vma=False,
    )
```
